256 devices in a mesh: seq: 64 (over z, y, core), tp: 4 (over x).
Axes of the slice: x: 4, y: 4, z: 8, core: 2. Of those that a mesh axis runs over, the one named last changes fastest.
Arguments:
- tokens: bfloat16 [16384, 2048], P('seq', 'tp'), may hold values from -6 to 6
- norm_gain: float32 [2048], replicated, may hold values from 0.1 to 1.9
- w_query: bfloat16 [2048, 1024], P(None, 'tp'), may hold values from -0.125 to 0.125
- w_key: bfloat16 [2048, 1024], P(None, 'tp'), may hold values from -0.125 to 0.125
- w_value: bfloat16 [2048, 2048], P(None, 'tp'), may hold values from -0.125 to 0.125
- w_gate_out: bfloat16 [2048, 2048], P(None, 'tp'), may hold values from -0.125 to 0.125
- gate_down: bfloat16 [2048, 16], replicated, may hold values from -0.09272438 to 0.09272438
- gate_up: bfloat16 [16, 1024], P(None, 'tp'), may hold values from -1 to 1.2625
- gate_bias: float32 [1024], P('tp'), may hold values from 1 to 8
- head_gain: float32 [2048], P('tp'), may hold values from 0.1 to 1.9
- w_out: bfloat16 [2048, 2048], P('tp'), may hold values from -0.125 to 0.125
- request_ids: int32 [16384], P('seq'), may hold values from 0 to 17, as said below
Outputs:
- mixed: bfloat16 [16384, 2048], P('seq', 'tp')
The draws below stay inside these ranges and needn't reach their ends.
Inputs may be any that keep to these rules, and one draw needn't show every extreme that they name: `request_ids`: request numbers never fall along the tokens; every request of 0 to 17 holds 1 to 8192 tokens; request 0 holds fewer than 256 tokens and request 1 holds exactly 8192.
All inputs are finite; a program needn't handle non-finite values.
Results may differ from the reference program's by a relative error of at most 0.015.
Values may be sent and summed in bfloat16 or wider, within the bound.
No kernel may reach another device: no remote copies, remote signals or barrier semaphores. Data moves between devices by JAX's collectives and lax.ppermute only.
A program may use at most 128 MiB of HBM per device.

```python
import jax
import jax.numpy as jnp
from jax import lax

D = 2048
H = 4
K = 256
V = 512
R = 16
C = 64
TOK_DEV = 256
TOKEN_COUNT = 16384
MAXLEN = 8192
REQUEST_COUNT = 18


def shared_direction(key):
    bits = jax.random.randint(jax.random.fold_in(key, 11), (D,), 0, 2, dtype=jnp.int32)
    return (2 * bits - 1).astype(jnp.float32)


def request_layout(key):
    others = REQUEST_COUNT - 2
    head_length = jax.random.randint(jax.random.fold_in(key, 24), (), 1, TOK_DEV, dtype=jnp.int32)
    first = jax.random.randint(jax.random.fold_in(key, 21), (others,), 1, 33, dtype=jnp.int32)
    second = jax.random.randint(jax.random.fold_in(key, 22), (others,), 1, 33, dtype=jnp.int32)
    shares = first * second
    spare = (MAXLEN - head_length - others).astype(jnp.int32)
    total = jnp.sum(shares).astype(jnp.int32)
    base = (spare * shares // total).astype(jnp.int32)
    rest = (spare - jnp.sum(base)).astype(jnp.int32)
    order = jnp.arange(others, dtype=jnp.int32)
    other_lengths = (1 + base + (order < rest).astype(jnp.int32)).astype(jnp.int32)
    index = jnp.arange(REQUEST_COUNT, dtype=jnp.int32)
    tail = other_lengths[jnp.clip(index - 2, 0, others - 1)]
    lengths = jnp.where(index == 0, head_length, jnp.where(index == 1, MAXLEN, tail)).astype(jnp.int32)
    ends = jnp.cumsum(lengths).astype(jnp.int32)
    position = jnp.arange(TOKEN_COUNT, dtype=jnp.int32)
    ids = jnp.sum((position[:, None] >= ends[None, :]).astype(jnp.int32), axis=1)
    return ids.astype(jnp.int32)


def request_lift(key, ids):
    chosen = jax.random.randint(jax.random.fold_in(key, 31), (REQUEST_COUNT,), 0, 2, dtype=jnp.int32).astype(jnp.float32)
    amount = jax.random.uniform(jax.random.fold_in(key, 33), (REQUEST_COUNT,), jnp.float32, 0.8, 1.2)
    return (chosen * amount)[ids]


def draw_request_ids(key, part):
    return request_layout(key)


def draw_tokens(key, part):
    ids = request_layout(key)
    lift = request_lift(key, ids)
    direction = shared_direction(key)
    noise_key = jax.random.fold_in(key, 41)
    noise = jax.random.truncated_normal(noise_key, -5.5, 5.5, (TOKEN_COUNT, D), jnp.float32)
    values = 0.98 * noise + 0.15 * lift[:, None] * direction[None, :]
    return values.astype(jnp.bfloat16)


def draw_gate_down(key, part):
    direction = shared_direction(key)
    noise = jax.random.truncated_normal(jax.random.fold_in(key, 51), -4.0, 4.0, (D, R), jnp.float32) * D ** (-0.5)
    return (noise + 7.0 / D * direction[:, None]).astype(jnp.bfloat16)


def draw_gate_up(key, part):
    noise = jax.random.truncated_normal(jax.random.fold_in(key, 61), -4.0, 4.0, (R, H * K), jnp.float32) * R ** (-0.5)
    lift = jax.random.uniform(jax.random.fold_in(key, 63), (H * K,), jnp.float32, 1.5, 4.0)
    return (noise + lift[None, :] / R).astype(jnp.bfloat16)


def draw_gate_bias(key, part):
    return jax.random.uniform(jax.random.fold_in(key, 71), (H * K,), jnp.float32, 1.0, 5.0)


def steps_of(own_key, shape, cuts, low, top_value):
    def one(dim, shards_of):
        draws = jax.random.uniform(jax.random.fold_in(jax.random.fold_in(own_key, 6), dim), (shards_of,), jnp.float32, low / len(cuts), top_value / len(cuts))
        return jnp.repeat(jnp.exp(draws), shape[dim] // shards_of).reshape((-1,) + (1,) * (len(shape) - dim - 1))

    level = one(*cuts[0])
    for cut in cuts[1:]:
        level = level * one(*cut)
    return level


def scatter_about(stream_key, dims, scale, limit, split=(), kind=jnp.bfloat16):
    values = scale * jax.random.normal(stream_key, dims, jnp.float32)
    if split:
        values = values * steps_of(stream_key, dims, split, -0.22, 0.18)
    return jnp.clip(values, -limit, limit).astype(kind)


def setup_inputs(seed: int = 0) -> dict:
    splits = jax.random.split(jax.random.key(seed), 13)
    return {
        "tokens": draw_tokens(jax.random.fold_in(splits[12], 71), 0),
        "norm_gain": jnp.clip(1.0 + 0.18 * jax.random.normal(splits[1], (D,), jnp.float32), 0.1, 1.9),
        "w_query": scatter_about(splits[2], (D, H * K), D ** -0.5, 0.125, ((1, 4),)),
        "w_key": scatter_about(splits[3], (D, H * K), D ** -0.5, 0.125, ((1, 4),)),
        "w_value": scatter_about(splits[4], (D, H * V), D ** -0.5, 0.125, ((1, 4),)),
        "w_gate_out": scatter_about(splits[5], (D, H * V), D ** -0.5, 0.125, ((1, 4),)),
        "gate_down": draw_gate_down(jax.random.fold_in(splits[12], 71), 0),
        "gate_up": draw_gate_up(jax.random.fold_in(splits[12], 71), 0),
        "gate_bias": draw_gate_bias(jax.random.fold_in(splits[12], 71), 0),
        "head_gain": jnp.clip(1.0 + 0.18 * jax.random.normal(splits[9], (H * V,), jnp.float32), 0.1, 1.9),
        "w_out": scatter_about(splits[10], (H * V, D), (H * V) ** -0.5, 0.125, ((0, 4),)),
        "request_ids": draw_request_ids(jax.random.fold_in(splits[12], 71), 0),
    }


def rms(value, gain):
    return value * lax.rsqrt(lax.optimization_barrier(jnp.mean(value * value, axis=-1, keepdims=True)) + 1e-05) * gain

def group_terms(query, key, value, log_decay_rate, ids, prev):
    cum = jnp.cumsum(log_decay_rate, axis=0)
    query_decayed = (query.astype(jnp.float32) * jnp.exp(cum) * K ** (-0.5)).astype(jnp.bfloat16)
    kinv = (key.astype(jnp.float32) * jnp.exp(-cum)).astype(jnp.bfloat16)
    scores = jnp.dot(query_decayed, kinv.T, preferred_element_type=jnp.float32)
    place = jnp.arange(query.shape[0], dtype=jnp.int32)
    allowed = (place[None, :] <= place[:, None]) & (ids[None, :] == ids[:, None])
    weights = jnp.where(allowed, scores, 0.0).astype(jnp.bfloat16)
    intra = jnp.dot(weights, value, preferred_element_type=jnp.float32)
    causal_mask = ids == prev
    keep = (ids == ids[-1]).astype(jnp.float32)[:, None]
    kend = (key.astype(jnp.float32) * jnp.exp(cum[-1:] - cum) * keep).astype(jnp.bfloat16)
    fresh = jnp.dot(kend.T, value, preferred_element_type=jnp.float32)
    decay = jnp.exp(cum[-1]) * (ids[-1] == prev).astype(jnp.float32)
    return (query_decayed, intra, causal_mask, fresh, decay)

def reference(tokens, norm_gain, w_query, w_key, w_value, w_gate_out, gate_down, gate_up, gate_bias, head_gain, w_out, request_ids):
    normed = rms(tokens.astype(jnp.float32), norm_gain).astype(jnp.bfloat16)
    low = jnp.dot(normed, gate_down, preferred_element_type=jnp.float32).astype(jnp.bfloat16)
    log_decay_rate = jax.nn.log_sigmoid(jnp.dot(low, gate_up, preferred_element_type=jnp.float32) + gate_bias) / 16.0
    query = jnp.dot(normed, w_query, preferred_element_type=jnp.float32).astype(jnp.bfloat16)
    key = jnp.dot(normed, w_key, preferred_element_type=jnp.float32).astype(jnp.bfloat16)
    value = jnp.dot(normed, w_value, preferred_element_type=jnp.float32).astype(jnp.bfloat16)
    opengate = jnp.dot(normed, w_gate_out, preferred_element_type=jnp.float32)
    blocks = TOKEN_COUNT // C
    request_id_block = request_ids.reshape(blocks, C)
    results = []
    for head in range(H):
        qh = query[:, head * K:(head + 1) * K].reshape(blocks, C, K)
        kh = key[:, head * K:(head + 1) * K].reshape(blocks, C, K)
        vh = value[:, head * V:(head + 1) * V].reshape(blocks, C, V)
        gh = log_decay_rate[:, head * K:(head + 1) * K].reshape(blocks, C, K)

        def step(carry, item):
            state, prev = carry
            qc, kc, vc, gc, sc = item
            query_decayed, intra, causal_mask, fresh, decay = group_terms(qc, kc, vc, gc, sc, prev)
            inter = jnp.dot(query_decayed.astype(jnp.float32), state, precision=lax.Precision.HIGHEST)
            attn = intra + jnp.where(causal_mask[:, None], inter, 0.0)
            return ((decay[:, None] * state + fresh, sc[-1]), attn)
        start = (jnp.zeros((K, V), jnp.float32), jnp.array(-1, jnp.int32))
        _, attn = lax.scan(step, start, (qh, kh, vh, gh, request_id_block))
        attn = attn.reshape(TOKEN_COUNT, V)
        gated = rms(attn, head_gain[head * V:(head + 1) * V]) * jax.nn.silu(opengate[:, head * V:(head + 1) * V])
        results.append(gated.astype(jnp.bfloat16))
    gated_all = jnp.concatenate(results, axis=1)
    return jnp.dot(gated_all, w_out, preferred_element_type=jnp.float32).astype(jnp.bfloat16)
```

```python
import jax
import jax.numpy as jnp
from jax import lax
from jax.experimental import pallas as pl
from jax.experimental.pallas import tpu as pltpu
from jax.sharding import PartitionSpec as P

K = 256
V = 512
C = 64
F = 512
HALF = 256
QUARTER = 64
META = 16
F32 = jnp.float32
BF = jnp.bfloat16
VM = pl.BlockSpec(memory_space=pltpu.VMEM)
SM = pl.BlockSpec(memory_space=pltpu.SMEM)


def dot(a, b, dims=((1,), (0,))):
    return lax.dot_general(a, b, (dims, ((), ())), preferred_element_type=F32)


def place():
    seq = lax.axis_index("seq")
    return lax.div(seq, 8), lax.rem(lax.div(seq, 2), 4), lax.rem(seq, 2)


def at(index, size):
    return pl.ds(pl.multiple_of(index * size, size), size)


def turn(index, distance):
    return lax.rem(index + distance, 4)


def load(ref):
    rows = ref.shape[0] - META
    state = ref[0:rows].astype(F32)
    meta = ref[rows:].astype(F32)
    return state, meta[0:1] + meta[1:2], meta[2:3], meta[3:4]


def meta_of(decay, first, last):
    high = decay.astype(BF).astype(F32)
    row = lax.broadcasted_iota(jnp.int32, (META, K), 0)
    meta = jnp.where(row == 0, high, jnp.where(row == 1, decay - high, 0.0))
    meta = jnp.where(row == 2, first, jnp.where(row == 3, last, meta))
    return meta.astype(BF)


def save(ref, element):
    state, decay, first, last = element
    rows = state.shape[0]
    ref[0:rows] = state.astype(BF)
    ref[rows:] = meta_of(decay, first, last)


def joined(earlier, later):
    factor = jnp.where(later[2] == earlier[3], later[1], 0.0)
    return (later[0] + factor * earlier[0], factor * earlier[1], earlier[2], later[3])


def pick(cond, a, b):
    return jax.tree.map(lambda u, v: jnp.where(cond, u, v), a, b)


def block_cumsum(rate):
    row = lax.broadcasted_iota(jnp.int32, (4 * C, 4 * C), 0)
    col = lax.broadcasted_iota(jnp.int32, (4 * C, 4 * C), 1)
    mask = ((row >= col) & (row // C == col // C)).astype(BF)
    one = rate.astype(BF)
    rest = rate - one.astype(F32)
    two = rest.astype(BF)
    three = (rest - two.astype(F32)).astype(BF)
    return dot(mask, three) + dot(mask, two) + dot(mask, one)


def front_kernel(t0, t1, t2, t3, gain, wk, wv, gd, gu, bias, idc, ids,
                 normed, key_o, value_o, cum_o, keep_o, send_o):
    x = lax.axis_index("tp")
    _, _, c = place()
    parts = [(t0, x), (t1, turn(x, 3)), (t2, turn(x, 1)), (t3, turn(x, 2))]
    squares = 0.0
    for ref, _ in parts:
        wide = ref[...].astype(F32)
        squares = squares + jnp.sum(wide * wide, axis=1, keepdims=True)
    scale = lax.rsqrt(squares * (1.0 / 2048) + 1e-05)
    key, value, low = 0.0, 0.0, 0.0
    for ref, owner in parts:
        part = (ref[...].astype(F32) * scale * gain[owner]).astype(BF)
        normed[owner] = part
        key = key + dot(part, wk[at(owner, F), :])
        value = value + dot(part, wv[at(owner, F), :])
        low = low + dot(part, gd[:, at(owner, F)], ((1,), (1,)))
    rate = dot(low.astype(BF), gu[...]) + bias[...]
    rate = (jnp.minimum(rate, 0.0) - jnp.log1p(jnp.exp(-jnp.abs(rate)))) * (1.0 / 16)
    key = key.astype(BF)
    key_o[...] = key
    value_o[...] = value.astype(BF)
    cum = block_cumsum(rate)
    cum_o[...] = cum
    ends = [cum[C * b + C - 1:C * b + C] for b in range(4)]
    after = [ends[1] + ends[2] + ends[3], ends[2] + ends[3], ends[3], jnp.zeros_like(ends[3])]
    first, last = ids[0], ids[4 * C - 1]
    keep = (idc[...] == last).astype(F32)
    ending = []
    for b in range(4):
        rows = slice(C * b, C * b + C)
        left = jnp.exp(after[b] + (ends[b] - cum[rows]))
        ending.append((key[rows].astype(F32) * left * keep[rows]).astype(BF))
    ending = jnp.concatenate(ending, axis=0)
    decay = jnp.exp(ends[0] + after[0])
    decay = jnp.where(first == last, decay, 0.0)
    meta = meta_of(decay, first.astype(F32), last.astype(F32))
    for ref, side in ((keep_o, c), (send_o, 1 - c)):
        ref[0:HALF] = dot(value_o[:, at(side, HALF)], ending, ((0,), (0,))).astype(BF)
        ref[HALF:] = meta


def inner_kernel(normed, wq, wg, key_r, value_r, cum_r, idc, idr, head_gain,
                 query_o, attn_o, gate_o):
    query, gate = 0.0, 0.0
    for i in range(4):
        part = normed[i]
        query = query + dot(part, wq[i * F:(i + 1) * F, :])
        gate = gate + dot(part, wg[i * F:(i + 1) * F, :])
    gate_o[...] = gate / (1.0 + jnp.exp(-gate)) * head_gain[...]
    query = query.astype(BF).astype(F32) * (K ** -0.5)
    key = key_r[...].astype(F32)
    cum = cum_r[...]
    ends = [cum[C * b + C - 1:C * b + C] for b in range(4)]
    before = [jnp.zeros_like(ends[0])]
    for b in range(3):
        before.append(before[-1] + ends[b])
    total = [before[b] + cum[C * b:C * b + C] for b in range(4)]
    for b in range(4):
        rows = slice(C * b, C * b + C)
        query_o[rows] = (query[rows] * jnp.exp(total[b])).astype(BF)
        decayed = (query[rows] * jnp.exp(cum[rows])).astype(BF)
        keys = [(key[C * j:C * j + C] * jnp.exp(before[b] - total[j])).astype(BF) for j in range(b)]
        keys.append((key[rows] * jnp.exp(-cum[rows])).astype(BF))
        keys = jnp.concatenate(keys, axis=0)
        scores = dot(decayed, keys, ((1,), (1,)))
        row = lax.broadcasted_iota(jnp.int32, scores.shape, 0) + C * b
        col = lax.broadcasted_iota(jnp.int32, scores.shape, 1)
        allowed = (col <= row) & (idr[:, 0:C * b + C] == idc[rows])
        weights = jnp.where(allowed, scores, 0.0).astype(BF)
        attn_o[rows] = dot(weights, value_r[0:C * b + C])


def pair_kernel(mine, other, own, s1, s2, s3, scratch):
    _, y, c = place()
    a, b = load(mine), load(other)
    total = joined(pick(c == 0, a, b), pick(c == 0, b, a))
    scratch[...] = total[0].astype(BF)
    meta = meta_of(*total[1:])
    for ref, d in ((own, 0), (s1, 1), (s2, 3), (s3, 2)):
        ref[0:QUARTER] = scratch[at(turn(y, d), QUARTER), :]
        ref[QUARTER:] = meta


def stack_rows(parts, stack):
    _, y, _ = place()
    for ref, d in zip(parts, (0, 3, 1, 2)):
        stack[turn(y, d)] = ref[...]
    return [load(stack.at[i]) for i in range(4)]


def row_kernel(own, r1, r2, r3, total, stack):
    chips = stack_rows((own, r1, r2, r3), stack)
    run = chips[0]
    for chip in chips[1:]:
        run = joined(run, chip)
    save(total, run)


def two_rows_kernel(row, before, total):
    save(total, joined(load(before), load(row)))


def spread_kernel(own, r1, r2, r3, one, two, far, own_o, s1, s2, s3, stack):
    _, y, _ = place()
    chips = stack_rows((own, r1, r2, r3), stack)
    run = joined(joined(load(far), load(two)), load(one))
    for i in range(4):
        save(stack.at[i], run)
        run = joined(run, chips[i])
    for ref, d in ((own_o, 0), (s1, 1), (s2, 3), (s3, 2)):
        ref[...] = stack[turn(y, d)]


def unpair_kernel(own, r1, r2, r3, mine, other, keep, send, scratch):
    _, y, c = place()
    for ref, d in zip((own, r1, r2, r3), (0, 3, 1, 2)):
        scratch[at(turn(y, d), QUARTER), :] = ref[0:QUARTER]
    meta = own[QUARTER:].astype(F32)
    into = (scratch[...].astype(F32), meta[0:1] + meta[1:2], meta[2:3], meta[3:4])
    after = joined(into, pick(c == 0, load(mine), load(other)))
    save(keep, pick(c == 0, into, after))
    save(send, pick(c == 0, after, into))


def back_kernel(mine, other, query, attn_r, gate, idc, w_out, own, s1, s2, s3, attn):
    x = lax.axis_index("tp")
    _, _, c = place()
    prev = mine[HALF:].astype(F32)[3:4, 0:1]
    seen = idc[...].astype(F32) == prev
    for ref, side in ((mine, c), (other, 1 - c)):
        inter = dot(query[...], ref[0:HALF], ((1,), (1,)))
        attn[:, at(side, HALF)] = attn_r[:, at(side, HALF)] + jnp.where(seen, inter, 0.0)
    full = attn[...]
    scale = lax.rsqrt(jnp.mean(full * full, axis=1, keepdims=True) + 1e-05)
    gated = (full * scale * gate[...]).astype(BF)
    for ref, d in ((s3, 2), (s1, 1), (s2, 3), (own, 0)):
        ref[...] = dot(gated, w_out[:, at(turn(x, d), F)]).astype(ref.dtype)


def call(kernel, outs, args, specs=None, scratch=(), flops=0, name=None):
    shapes = [jax.ShapeDtypeStruct(s, d) for s, d in outs]
    bytes_accessed = sum(a.size * a.dtype.itemsize for a in list(args) + shapes)
    return pl.pallas_call(
        kernel,
        out_shape=shapes,
        in_specs=specs or [VM] * len(args),
        out_specs=[VM] * len(outs),
        scratch_shapes=list(scratch),
        compiler_params=pltpu.CompilerParams(vmem_limit_bytes=24 << 20),
        cost_estimate=pl.CostEstimate(flops=flops, bytes_accessed=bytes_accessed, transcendentals=0),
        name=name,
    )(*args)


def over_tp(block, distance):
    return lax.ppermute(block, "tp", [(i, (i + distance) % 4) for i in range(4)])


def seq_route(move):
    pairs = []
    for i in range(64):
        z, y, c = move(i // 8, i // 2 % 4, i % 2)
        if z < 8:
            pairs.append((i, z * 8 + y * 2 + c))
    return pairs


def over_seq(block, move):
    return lax.ppermute(block, "seq", seq_route(move))


def over_y(blocks):
    return [
        over_seq(b, lambda z, y, c, d=d: (z, (y + d) % 4, c)) for b, d in zip(blocks, (1, 3, 2))
    ]


def swap(block):
    return over_seq(block, lambda z, y, c: (z, y, 1 - c))


def per_device(tokens, norm_gain, w_query, w_key, w_value, w_gate_out, gate_down, gate_up,
               gate_bias, head_gain, w_out, request_ids):
    rows = tokens.shape[0]
    t3 = over_tp(tokens, 2)
    t1 = over_tp(tokens, 1)
    t2 = over_tp(tokens, 3)
    idc, idr = request_ids.reshape(rows, 1), request_ids.reshape(1, rows)
    piece = (QUARTER + META, K)
    half = (HALF + META, K)
    normed, key, value, cum, mine, send = call(
        front_kernel,
        [((4, rows, F), BF), ((rows, K), BF), ((rows, V), BF), ((rows, K), F32), (half, BF), (half, BF)],
        (tokens, t1, t2, t3, norm_gain.reshape(4, 1, F), w_key, w_value, gate_down.T, gate_up,
         gate_bias.reshape(1, K), idc, request_ids),
        specs=[VM] * 11 + [SM], flops=2 * rows * 2048 * 784, name="front")
    other = swap(send)
    query, attn, gate = call(
        inner_kernel,
        [((rows, K), BF), ((rows, V), F32), ((rows, V), F32)],
        (normed, w_query, w_gate_out, key, value, cum, idc, idr, head_gain.reshape(1, V)),
        flops=2 * rows * 2048 * 1024, name="inner")
    own, s1, s2, s3 = call(pair_kernel, [(piece, BF)] * 4, (mine, other),
                           scratch=[pltpu.VMEM((HALF, K), BF)], name="pair")
    chips = [own] + over_y((s1, s2, s3))
    row, = call(row_kernel, [(piece, BF)], chips, scratch=[pltpu.VMEM((4,) + piece, BF)], name="row")
    one = over_seq(row, lambda z, y, c: (z + 1, y, c))
    far = over_seq(row, lambda z, y, c: (4 if z == 0 else 8, y, c))
    pair, = call(two_rows_kernel, [(piece, BF)], (row, one), name="two_rows")
    two = over_seq(pair, lambda z, y, c: (z + 2, y, c))
    own, s1, s2, s3 = call(spread_kernel, [(piece, BF)] * 4, (*chips, one, two, far),
                           scratch=[pltpu.VMEM((4,) + piece, BF)], name="spread")
    keep, send = call(unpair_kernel, [(half, BF)] * 2, (own, *over_y((s1, s2, s3)), mine, other),
                      scratch=[pltpu.VMEM((HALF, K), BF)], name="unpair")
    own, s1, s2, s3 = call(
        back_kernel, [((rows, F), F32)] + [((rows, F), BF)] * 3,
        (keep, swap(send), query, attn, gate, idc, w_out),
        scratch=[pltpu.VMEM((rows, V), F32)], flops=2 * rows * V * 2304, name="back")
    p3 = over_tp(s3, 2)
    p1 = over_tp(s1, 1)
    p2 = over_tp(s2, 3)
    return (own + p1.astype(F32) + p2.astype(F32) + p3.astype(F32)).astype(BF)


def solution(mesh):
    return jax.shard_map(
        per_device,
        mesh=mesh,
        in_specs=(
            P("seq", "tp"),
            P(),
            P(None, "tp"),
            P(None, "tp"),
            P(None, "tp"),
            P(None, "tp"),
            P(),
            P(None, "tp"),
            P("tp"),
            P("tp"),
            P("tp", None),
            P("seq"),
        ),
        out_specs=P("seq", "tp"),
        check_vma=False,
    )
```

```python
import jax
import jax.numpy as jnp
from jax import lax
from jax.experimental import pallas as pl
from jax.experimental.pallas import tpu as pltpu
from jax.sharding import PartitionSpec as P

K = 256
V = 512
C = 64
F = 512
HALF = 256
QUARTER = 64
META = 16
F32 = jnp.float32
BF = jnp.bfloat16
VM = pl.BlockSpec(memory_space=pltpu.VMEM)
HBM = pl.BlockSpec(memory_space=pltpu.HBM)


def dot(a, b, dims=((1,), (0,))):
    return lax.dot_general(a, b, (dims, ((), ())), preferred_element_type=F32)


def place():
    seq = lax.axis_index("seq")
    return lax.div(seq, 8), lax.rem(lax.div(seq, 2), 4), lax.rem(seq, 2)


def at(index, size):
    return pl.ds(pl.multiple_of(index * size, size), size)


FLIPS = (0, 2, 1, 3)


def flip(index, bits):
    return lax.bitwise_xor(index, bits)


def load(ref):
    rows = ref.shape[0] - META
    state = ref[0:rows].astype(F32)
    meta = ref[rows:].astype(F32)
    return state, meta[0:1] + meta[1:2], meta[2:3], meta[3:4]


def meta_of(decay, first, last):
    high = decay.astype(BF).astype(F32)
    row = lax.broadcasted_iota(jnp.int32, (META, K), 0)
    meta = jnp.where(row == 0, high, jnp.where(row == 1, decay - high, 0.0))
    meta = jnp.where(row == 2, first, jnp.where(row == 3, last, meta))
    return meta.astype(BF)


def save(ref, element):
    state, decay, first, last = element
    rows = state.shape[0]
    ref[0:rows] = state.astype(BF)
    ref[rows:] = meta_of(decay, first, last)


def joined(earlier, later):
    factor = jnp.where(later[2] == earlier[3], later[1], 0.0)
    return (later[0] + factor * earlier[0], factor * earlier[1], earlier[2], later[3])


def pick(cond, a, b):
    return jax.tree.map(lambda u, v: jnp.where(cond, u, v), a, b)


def block_cumsum(rate):
    row = lax.broadcasted_iota(jnp.int32, (4 * C, 4 * C), 0)
    col = lax.broadcasted_iota(jnp.int32, (4 * C, 4 * C), 1)
    mask = ((row >= col) & (row // C == col // C)).astype(BF)
    one = rate.astype(BF)
    rest = rate - one.astype(F32)
    two = rest.astype(BF)
    three = (rest - two.astype(F32)).astype(BF)
    return dot(mask, three) + dot(mask, two) + dot(mask, one)


def stage_kernel(*refs):
    count = len(refs) // 2
    done = refs[-1]
    copies = [pltpu.make_async_copy(refs[i], refs[count + i], done.at[i]) for i in range(count)]
    for copy in copies:
        copy.start()
    for copy in copies:
        copy.wait()


def front_kernel(t0, t1, t2, t3, gain, wk, wv, gd, gu, bias, idc,
                 normed, key_o, value_o, cum_o, keep_o, send_o):
    x = lax.axis_index("tp")
    _, _, c = place()
    parts = [(ref, flip(x, d)) for d, ref in zip(FLIPS, (t0, t1, t2, t3))]
    squares = 0.0
    for ref, _ in parts:
        wide = ref[...].astype(F32)
        squares = squares + jnp.sum(wide * wide, axis=1, keepdims=True)
    scale = lax.rsqrt(squares * (1.0 / 2048) + 1e-05)
    key, value, low = 0.0, 0.0, 0.0
    for ref, owner in parts:
        part = (ref[...].astype(F32) * scale * gain[owner]).astype(BF)
        normed[owner] = part
        key = key + dot(part, wk[at(owner, F), :])
        value = value + dot(part, wv[at(owner, F), :])
        low = low + dot(part, gd[:, at(owner, F)], ((1,), (1,)))
    rate = dot(low.astype(BF), gu[...]) + bias[...]
    rate = (jnp.minimum(rate, 0.0) - jnp.log1p(jnp.exp(-jnp.abs(rate)))) * (1.0 / 16)
    key = key.astype(BF)
    key_o[...] = key
    value_o[...] = value.astype(BF)
    cum = block_cumsum(rate)
    cum_o[...] = cum
    ends = [cum[C * b + C - 1:C * b + C] for b in range(4)]
    after = [ends[1] + ends[2] + ends[3], ends[2] + ends[3], ends[3], jnp.zeros_like(ends[3])]
    ids = idc[...].astype(F32)
    first, last = ids[0:1], ids[4 * C - 1:]
    keep = (ids == last).astype(F32)
    ending = []
    for b in range(4):
        rows = slice(C * b, C * b + C)
        left = jnp.exp(after[b] + (ends[b] - cum[rows]))
        ending.append((key[rows].astype(F32) * left * keep[rows]).astype(BF))
    ending = jnp.concatenate(ending, axis=0)
    decay = jnp.exp(ends[0] + after[0])
    decay = jnp.where(first == last, decay, 0.0)
    meta = meta_of(decay, first, last)
    for ref, side in ((keep_o, c), (send_o, 1 - c)):
        ref[0:HALF] = dot(value_o[:, at(side, HALF)], ending, ((0,), (0,))).astype(BF)
        ref[HALF:] = meta


def inner_kernel(normed, wq, wg, key_r, value_r, cum_r, idc, idr, head_gain,
                 query_o, attn_o, gate_o):
    query, gate = 0.0, 0.0
    for i in range(4):
        part = normed[i]
        query = query + dot(part, wq[i * F:(i + 1) * F, :])
        gate = gate + dot(part, wg[i * F:(i + 1) * F, :])
    gate_o[...] = gate / (1.0 + jnp.exp(-gate)) * head_gain[...]
    query = query.astype(BF).astype(F32) * (K ** -0.5)
    key = key_r[...].astype(F32)
    cum = cum_r[...]
    ends = [cum[C * b + C - 1:C * b + C] for b in range(4)]
    before = [jnp.zeros_like(ends[0])]
    for b in range(3):
        before.append(before[-1] + ends[b])
    total = [before[b] + cum[C * b:C * b + C] for b in range(4)]
    for b in range(4):
        rows = slice(C * b, C * b + C)
        query_o[rows] = (query[rows] * jnp.exp(total[b])).astype(BF)
        decayed = (query[rows] * jnp.exp(cum[rows])).astype(BF)
        keys = [(key[C * j:C * j + C] * jnp.exp(before[b] - total[j])).astype(BF) for j in range(b)]
        keys.append((key[rows] * jnp.exp(-cum[rows])).astype(BF))
        keys = jnp.concatenate(keys, axis=0)
        scores = dot(decayed, keys, ((1,), (1,)))
        row = lax.broadcasted_iota(jnp.int32, scores.shape, 0) + C * b
        col = lax.broadcasted_iota(jnp.int32, scores.shape, 1)
        allowed = (col <= row) & (idr[:, 0:C * b + C] == idc[rows])
        weights = jnp.where(allowed, scores, 0.0).astype(BF)
        attn_o[rows] = dot(weights, value_r[0:C * b + C])


def pair_kernel(mine, other, own, s1, s2, s3, scratch):
    _, y, c = place()
    a, b = load(mine), load(other)
    total = joined(pick(c == 0, a, b), pick(c == 0, b, a))
    scratch[...] = total[0].astype(BF)
    meta = meta_of(*total[1:])
    for d, ref in zip(FLIPS, (own, s1, s2, s3)):
        ref[0:QUARTER] = scratch[at(flip(y, d), QUARTER), :]
        ref[QUARTER:] = meta


def stack_rows(parts, stack):
    _, y, _ = place()
    for d, ref in zip(FLIPS, parts):
        stack[flip(y, d)] = ref[...]
    return [load(stack.at[i]) for i in range(4)]


def row_kernel(own, r1, r2, r3, total, stack):
    chips = stack_rows((own, r1, r2, r3), stack)
    run = chips[0]
    for chip in chips[1:]:
        run = joined(run, chip)
    save(total, run)


def two_rows_kernel(row, beside, total):
    z, _, _ = place()
    a, b = load(row), load(beside)
    odd = lax.rem(z, 2) == 1
    save(total, joined(pick(odd, b, a), pick(odd, a, b)))


def four_rows_kernel(pair, beside, total):
    save(total, joined(load(beside), load(pair)))


def spread_kernel(own, r1, r2, r3, z1, z2, z3, own_o, s1, s2, s3, stack):
    z, y, _ = place()
    chips = stack_rows((own, r1, r2, r3), stack)
    state, *rest = pick(z == 4, load(z3), load(z2))
    before = (jnp.where((lax.rem(z, 4) >= 2) | (z == 4), state, 0.0), *rest)
    run = pick(lax.rem(z, 2) == 1, joined(before, load(z1)), before)
    for i in range(4):
        save(stack.at[i], run)
        run = joined(run, chips[i])
    for d, ref in zip(FLIPS, (own_o, s1, s2, s3)):
        ref[...] = stack[flip(y, d)]


def unpair_kernel(own, r1, r2, r3, mine, other, keep, send, scratch):
    _, y, c = place()
    for d, ref in zip(FLIPS, (own, r1, r2, r3)):
        scratch[at(flip(y, d), QUARTER), :] = ref[0:QUARTER]
    meta = own[QUARTER:].astype(F32)
    into = (scratch[...].astype(F32), meta[0:1] + meta[1:2], meta[2:3], meta[3:4])
    after = joined(into, pick(c == 0, load(mine), load(other)))
    save(keep, pick(c == 0, into, after))
    save(send, pick(c == 0, after, into))


def back_kernel(mine, other, query, attn_r, gate, idc, w_out, gated_o, s2, attn):
    x = lax.axis_index("tp")
    _, _, c = place()
    prev = mine[HALF:].astype(F32)[3:4, 0:1]
    seen = idc[...].astype(F32) == prev
    for ref, side in ((mine, c), (other, 1 - c)):
        inter = dot(query[...], ref[0:HALF], ((1,), (1,)))
        attn[:, at(side, HALF)] = attn_r[:, at(side, HALF)] + jnp.where(seen, inter, 0.0)
    full = attn[...]
    scale = lax.rsqrt(jnp.mean(full * full, axis=1, keepdims=True) + 1e-05)
    gated_o[...] = (full * scale * gate[...]).astype(BF)
    s2[...] = dot(gated_o[...], w_out[:, at(flip(x, 2), F)]).astype(BF)


def beside_kernel(gated, w_out, s1, s3):
    x = lax.axis_index("tp")
    for d, ref in ((3, s3), (1, s1)):
        ref[...] = dot(gated[...], w_out[:, at(flip(x, d), F)]).astype(BF)


def here_kernel(gated, w_out, own):
    x = lax.axis_index("tp")
    own[...] = dot(gated[...], w_out[:, at(x, F)])


def call(kernel, outs, args, specs=None, scratch=(), flops=0, name=None, vmem=24):
    shapes = [jax.ShapeDtypeStruct(s, d) for s, d in outs]
    bytes_accessed = sum(a.size * a.dtype.itemsize for a in list(args) + shapes)
    return pl.pallas_call(
        kernel,
        out_shape=shapes,
        in_specs=specs or [VM] * len(args),
        out_specs=[VM] * len(outs),
        scratch_shapes=list(scratch),
        compiler_params=pltpu.CompilerParams(vmem_limit_bytes=vmem << 20),
        cost_estimate=pl.CostEstimate(flops=flops, bytes_accessed=bytes_accessed, transcendentals=0),
        name=name,
    )(*args)


def over_tp(block, bits):
    return lax.ppermute(block, "tp", [(i, i ^ bits) for i in range(4)])


def seq_route(move):
    route = []
    for i in range(64):
        z, y, c = move(i // 8, i // 2 % 4, i % 2)
        route.append((i, z * 8 + y * 2 + c))
    return route


def over_seq(block, move):
    return lax.ppermute(block, "seq", seq_route(move))


def over_y(blocks):
    return [
        over_seq(b, lambda z, y, c, d=d: (z, y ^ d, c)) for d, b in zip(FLIPS[1:], blocks)
    ]


def swap(block):
    return over_seq(block, lambda z, y, c: (z, y, 1 - c))


def per_device(tokens, norm_gain, w_query, w_key, w_value, w_gate_out, gate_down, gate_up,
               gate_bias, head_gain, w_out, request_ids):
    rows = tokens.shape[0]
    t1, t2, t3 = (over_tp(tokens, d) for d in FLIPS[1:])
    idc, idr = request_ids.reshape(rows, 1), request_ids.reshape(1, rows)
    piece = (QUARTER + META, K)
    half = (HALF + META, K)
    held = (tokens, norm_gain.reshape(4, 1, F), w_key, w_value, gate_down.T, gate_up,
            gate_bias.reshape(1, K))
    tokens, gain, w_key, w_value, down, up, bias = call(
        stage_kernel, [(a.shape, a.dtype) for a in held], held, specs=[HBM] * len(held),
        scratch=[pltpu.SemaphoreType.DMA((len(held),))], name="stage")
    normed, key, value, cum, mine, send = call(
        front_kernel,
        [((4, rows, F), BF), ((rows, K), BF), ((rows, V), BF), ((rows, K), F32), (half, BF), (half, BF)],
        (tokens, t1, t2, t3, gain, w_key, w_value, down, up, bias, idc),
        flops=2 * rows * 2048 * 784, name="front")
    other = swap(send)
    query, attn, gate = call(
        inner_kernel,
        [((rows, K), BF), ((rows, V), F32), ((rows, V), F32)],
        (normed, w_query, w_gate_out, key, value, cum, idc, idr, head_gain.reshape(1, V)),
        flops=2 * rows * 2048 * 1024, name="inner")
    own, s1, s2, s3 = call(pair_kernel, [(piece, BF)] * 4, (mine, other),
                           scratch=[pltpu.VMEM((HALF, K), BF)], name="pair")
    r1, r2, r3 = over_y((s1, s2, s3))
    r1, query = lax.optimization_barrier((r1, query))
    chips = [own, r1, r2, r3]
    row, = call(row_kernel, [(piece, BF)], chips, scratch=[pltpu.VMEM((4,) + piece, BF)], name="row")
    z1 = over_seq(row, lambda z, y, c: (z ^ 1, y, c))
    pair, = call(two_rows_kernel, [(piece, BF)], (row, z1), name="two_rows")
    z2 = over_seq(pair, lambda z, y, c: (z ^ 2, y, c))
    four, = call(four_rows_kernel, [(piece, BF)], (pair, z2), name="four_rows")
    z3 = over_seq(four, lambda z, y, c: ({3: 4, 4: 3}.get(z, z), y, c))
    own, s1, s2, s3 = call(spread_kernel, [(piece, BF)] * 4, (*chips, z1, z2, z3),
                           scratch=[pltpu.VMEM((4,) + piece, BF)], name="spread")
    keep, send = call(unpair_kernel, [(half, BF)] * 2, (own, *over_y((s1, s2, s3)), mine, other),
                      scratch=[pltpu.VMEM((HALF, K), BF)], name="unpair")
    gated, s2 = call(
        back_kernel, [((rows, V), BF), ((rows, F), BF)],
        (keep, swap(send), query, attn, gate, idc, w_out),
        scratch=[pltpu.VMEM((rows, V), F32)], flops=2 * rows * V * 768, name="back")
    p2 = over_tp(s2, 2)
    s1, s3 = call(beside_kernel, [((rows, F), BF)] * 2, (gated, w_out),
                  flops=4 * rows * V * F, name="beside")
    p1, p3 = over_tp(s1, 1), over_tp(s3, 3)
    own, = call(here_kernel, [((rows, F), F32)], (gated, w_out), flops=2 * rows * V * F, name="here")
    return (own + p1.astype(F32) + p2.astype(F32) + p3.astype(F32)).astype(BF)


def solution(mesh):
    return jax.shard_map(
        per_device,
        mesh=mesh,
        in_specs=(
            P("seq", "tp"),
            P(),
            P(None, "tp"),
            P(None, "tp"),
            P(None, "tp"),
            P(None, "tp"),
            P(),
            P(None, "tp"),
            P("tp"),
            P("tp"),
            P("tp", None),
            P("seq"),
        ),
        out_specs=P("seq", "tp"),
        check_vma=False,
    )
```

```python
import jax
import jax.numpy as jnp
from jax import lax
from jax.experimental import pallas as pl
from jax.experimental.pallas import tpu as pltpu
from jax.sharding import PartitionSpec as P

K = 256
V = 512
C = 64
F = 512
QUARTER = 128
META = 16
F32 = jnp.float32
BF = jnp.bfloat16
VM = pl.BlockSpec(memory_space=pltpu.VMEM)
HBM = pl.BlockSpec(memory_space=pltpu.HBM)


def dot(a, b, dims=((1,), (0,))):
    return lax.dot_general(a, b, (dims, ((), ())), preferred_element_type=F32)


def place():
    seq = lax.axis_index("seq")
    return lax.div(seq, 8), lax.rem(lax.div(seq, 2), 4), lax.rem(seq, 2)


def at(index, size):
    return pl.ds(pl.multiple_of(index * size, size), size)


FLIPS = (0, 2, 1, 3)


def flip(index, bits):
    return lax.bitwise_xor(index, bits)


def load(ref):
    rows = ref.shape[0] - META
    state = ref[0:rows].astype(F32)
    meta = ref[rows:].astype(F32)
    return state, meta[0:1] + meta[1:2], meta[2:3], meta[3:4]


def meta_of(decay, first, last):
    high = decay.astype(BF).astype(F32)
    row = lax.broadcasted_iota(jnp.int32, (META, K), 0)
    meta = jnp.where(row == 0, high, jnp.where(row == 1, decay - high, 0.0))
    meta = jnp.where(row == 2, first, jnp.where(row == 3, last, meta))
    return meta.astype(BF)


def save(ref, element):
    state, decay, first, last = element
    rows = state.shape[0]
    ref[0:rows] = state.astype(BF)
    ref[rows:] = meta_of(decay, first, last)


def joined(earlier, later):
    factor = jnp.where(later[2] == earlier[3], later[1], 0.0)
    return (later[0] + factor * earlier[0], factor * earlier[1], earlier[2], later[3])


def pick(cond, a, b):
    return jax.tree.map(lambda u, v: jnp.where(cond, u, v), a, b)


def block_cumsum(rate):
    row = lax.broadcasted_iota(jnp.int32, (4 * C, 4 * C), 0)
    col = lax.broadcasted_iota(jnp.int32, (4 * C, 4 * C), 1)
    mask = ((row >= col) & (row // C == col // C)).astype(BF)
    one = rate.astype(BF)
    rest = rate - one.astype(F32)
    two = rest.astype(BF)
    three = (rest - two.astype(F32)).astype(BF)
    return dot(mask, three) + dot(mask, two) + dot(mask, one)


def stage_kernel(*refs):
    count = len(refs) // 2
    done = refs[-1]
    copies = [pltpu.make_async_copy(refs[i], refs[count + i], done.at[i]) for i in range(count)]
    for copy in copies:
        copy.start()
    for copy in copies:
        copy.wait()


def front_kernel(t0, t1, t2, t3, gain, wk, wv, gd, gu, bias, idc,
                 normed, key_o, value_o, cum_o, element):
    x = lax.axis_index("tp")
    parts = [(ref, flip(x, d)) for d, ref in zip(FLIPS, (t0, t1, t2, t3))]
    squares = 0.0
    for ref, _ in parts:
        wide = ref[...].astype(F32)
        squares = squares + jnp.sum(wide * wide, axis=1, keepdims=True)
    scale = lax.rsqrt(squares * (1.0 / 2048) + 1e-05)
    key, value, low = 0.0, 0.0, 0.0
    for ref, owner in parts:
        part = (ref[...].astype(F32) * scale * gain[owner]).astype(BF)
        normed[owner] = part
        key = key + dot(part, wk[at(owner, F), :])
        value = value + dot(part, wv[at(owner, F), :])
        low = low + dot(part, gd[:, at(owner, F)], ((1,), (1,)))
    rate = dot(low.astype(BF), gu[...]) + bias[...]
    rate = (jnp.minimum(rate, 0.0) - jnp.log1p(jnp.exp(-jnp.abs(rate)))) * (1.0 / 16)
    key = key.astype(BF)
    key_o[...] = key
    value_o[...] = value.astype(BF)
    cum = block_cumsum(rate)
    cum_o[...] = cum
    ends = [cum[C * b + C - 1:C * b + C] for b in range(4)]
    after = [ends[1] + ends[2] + ends[3], ends[2] + ends[3], ends[3], jnp.zeros_like(ends[3])]
    ids = idc[...].astype(F32)
    first, last = ids[0:1], ids[4 * C - 1:]
    keep = (ids == last).astype(F32)
    ending = []
    for b in range(4):
        rows = slice(C * b, C * b + C)
        left = jnp.exp(after[b] + (ends[b] - cum[rows]))
        ending.append((key[rows].astype(F32) * left * keep[rows]).astype(BF))
    ending = jnp.concatenate(ending, axis=0)
    decay = jnp.exp(ends[0] + after[0])
    decay = jnp.where(first == last, decay, 0.0)
    element[0:V] = dot(value_o[...], ending, ((0,), (0,))).astype(BF)
    element[V:] = meta_of(decay, first, last)


def inner_kernel(normed, wq, wg, key_r, value_r, cum_r, idc, idr, head_gain,
                 query_o, attn_o, gate_o):
    query, gate = 0.0, 0.0
    for i in range(4):
        part = normed[i]
        query = query + dot(part, wq[i * F:(i + 1) * F, :])
        gate = gate + dot(part, wg[i * F:(i + 1) * F, :])
    gate_o[...] = gate / (1.0 + jnp.exp(-gate)) * head_gain[...]
    query = query.astype(BF).astype(F32) * (K ** -0.5)
    key = key_r[...].astype(F32)
    cum = cum_r[...]
    ends = [cum[C * b + C - 1:C * b + C] for b in range(4)]
    before = [jnp.zeros_like(ends[0])]
    for b in range(3):
        before.append(before[-1] + ends[b])
    total = [before[b] + cum[C * b:C * b + C] for b in range(4)]
    for b in range(4):
        rows = slice(C * b, C * b + C)
        query_o[rows] = (query[rows] * jnp.exp(total[b])).astype(BF)
        decayed = (query[rows] * jnp.exp(cum[rows])).astype(BF)
        keys = [(key[C * j:C * j + C] * jnp.exp(before[b] - total[j])).astype(BF) for j in range(b)]
        keys.append((key[rows] * jnp.exp(-cum[rows])).astype(BF))
        keys = jnp.concatenate(keys, axis=0)
        scores = dot(decayed, keys, ((1,), (1,)))
        row = lax.broadcasted_iota(jnp.int32, scores.shape, 0) + C * b
        col = lax.broadcasted_iota(jnp.int32, scores.shape, 1)
        allowed = (col <= row) & (idr[:, 0:C * b + C] == idc[rows])
        weights = jnp.where(allowed, scores, 0.0).astype(BF)
        attn_o[rows] = dot(weights, value_r[0:C * b + C])


def pair_kernel(mine, other, own, s1, s2, s3, scratch):
    _, y, _ = place()
    total = joined(load(other), load(mine))
    scratch[...] = total[0].astype(BF)
    meta = meta_of(*total[1:])
    for d, ref in zip(FLIPS, (own, s1, s2, s3)):
        ref[0:QUARTER] = scratch[at(flip(y, d), QUARTER), :]
        ref[QUARTER:] = meta


def stack_rows(parts, stack):
    _, y, _ = place()
    for d, ref in zip(FLIPS, parts):
        stack[flip(y, d)] = ref[...]
    return [load(stack.at[i]) for i in range(4)]


def row_kernel(own, r1, r2, r3, total, stack):
    chips = stack_rows((own, r1, r2, r3), stack)
    run = chips[0]
    for chip in chips[1:]:
        run = joined(run, chip)
    save(total, run)


def two_rows_kernel(row, beside, total):
    z, _, _ = place()
    a, b = load(row), load(beside)
    odd = lax.rem(z, 2) == 1
    save(total, joined(pick(odd, b, a), pick(odd, a, b)))


def spread_kernel(own, r1, r2, r3, z1, far3, far1, z2, own_o, s1, s2, s3, stack):
    z, y, _ = place()
    chips = stack_rows((own, r1, r2, r3), stack)
    state, *rest = pick(z == 4, joined(load(far1), load(far3)), load(z2))
    before = (jnp.where((lax.rem(z, 4) >= 2) | (z == 4), state, 0.0), *rest)
    run = pick(lax.rem(z, 2) == 1, joined(before, load(z1)), before)
    for i in range(4):
        save(stack.at[i], run)
        run = joined(run, chips[i])
    for d, ref in zip(FLIPS, (own_o, s1, s2, s3)):
        ref[...] = stack[flip(y, d)]


def unpair_kernel(own, r1, r2, r3, other, into, after):
    _, y, _ = place()
    for d, ref in zip(FLIPS, (own, r1, r2, r3)):
        into[at(flip(y, d), QUARTER), :] = ref[0:QUARTER]
    into[V:] = own[QUARTER:]
    save(after, joined(load(into), load(other)))


def back_kernel(after, into, query, attn_r, gate, idc, w_out, gated_o, s2):
    x = lax.axis_index("tp")
    _, _, c = place()
    before = jnp.where(c == 0, into[...].astype(F32), after[...].astype(F32))
    seen = idc[...].astype(F32) == before[V + 3:V + 4, 0:1]
    inter = dot(query[...], before[0:V].astype(BF), ((1,), (1,)))
    full = attn_r[...] + jnp.where(seen, inter, 0.0)
    scale = lax.rsqrt(jnp.mean(full * full, axis=1, keepdims=True) + 1e-05)
    gated_o[...] = (full * scale * gate[...]).astype(BF)
    s2[...] = dot(gated_o[...], w_out[:, at(flip(x, 2), F)]).astype(BF)


def beside_kernel(gated, w_out, s1, s3):
    x = lax.axis_index("tp")
    for d, ref in ((3, s3), (1, s1)):
        ref[...] = dot(gated[...], w_out[:, at(flip(x, d), F)]).astype(BF)


def here_kernel(gated, w_out, own):
    x = lax.axis_index("tp")
    own[...] = dot(gated[...], w_out[:, at(x, F)])


def call(kernel, outs, args, specs=None, scratch=(), flops=0, name=None, vmem=24):
    shapes = [jax.ShapeDtypeStruct(s, d) for s, d in outs]
    bytes_accessed = sum(a.size * a.dtype.itemsize for a in list(args) + shapes)
    return pl.pallas_call(
        kernel,
        out_shape=shapes,
        in_specs=specs or [VM] * len(args),
        out_specs=[VM] * len(outs),
        scratch_shapes=list(scratch),
        compiler_params=pltpu.CompilerParams(vmem_limit_bytes=vmem << 20),
        cost_estimate=pl.CostEstimate(flops=flops, bytes_accessed=bytes_accessed, transcendentals=0),
        name=name,
    )(*args)


def over_tp(block, bits):
    return lax.ppermute(block, "tp", [(i, i ^ bits) for i in range(4)])


def over_seq(block, move):
    route = []
    for i in range(64):
        z, y, c = move(i // 8, i // 2 % 4, i % 2)
        route.append((i, z * 8 + y * 2 + c))
    return lax.ppermute(block, "seq", route)


def over_chips(block, move):
    route = []
    for i in range(256):
        z, y, c, x = i // 32, i // 8 % 4, i // 4 % 2, i % 4
        z, y, x = (*move(z, y), x) if c else (z, y, x ^ 1)
        route.append((i, ((z * 4 + y) * 2 + c) * 4 + x))
    return lax.ppermute(block, ("seq", "tp"), route)


def to_row_4(block, z):
    return lax.ppermute(block, "seq", [(z * 8 + i, 32 + i) for i in range(1, 8, 2)])


def over_y(blocks):
    return [
        over_chips(b, lambda z, y, d=d: (z, y ^ d)) for d, b in zip(FLIPS[1:], blocks)
    ]


def swap(block):
    return over_seq(block, lambda z, y, c: (z, y, 1 - c))


def per_device(tokens, norm_gain, w_query, w_key, w_value, w_gate_out, gate_down, gate_up,
               gate_bias, head_gain, w_out, request_ids):
    rows = tokens.shape[0]
    t1, t2, t3 = (over_tp(tokens, d) for d in FLIPS[1:])
    idc, idr = request_ids.reshape(rows, 1), request_ids.reshape(1, rows)
    piece = (QUARTER + META, K)
    whole = (V + META, K)
    held = (tokens, norm_gain.reshape(4, 1, F), w_key, w_value, gate_down.T, gate_up,
            gate_bias.reshape(1, K))
    tokens, gain, w_key, w_value, down, up, bias = call(
        stage_kernel, [(a.shape, a.dtype) for a in held], held, specs=[HBM] * len(held),
        scratch=[pltpu.SemaphoreType.DMA((len(held),))], name="stage")
    normed, key, value, cum, mine = call(
        front_kernel,
        [((4, rows, F), BF), ((rows, K), BF), ((rows, V), BF), ((rows, K), F32), (whole, BF)],
        (tokens, t1, t2, t3, gain, w_key, w_value, down, up, bias, idc),
        flops=2 * rows * 2048 * 784, name="front")
    other = swap(mine)
    query, attn, gate = call(
        inner_kernel,
        [((rows, K), BF), ((rows, V), F32), ((rows, V), F32)],
        (normed, w_query, w_gate_out, key, value, cum, idc, idr, head_gain.reshape(1, V)),
        flops=2 * rows * 2048 * 1024, name="inner")
    own, s1, s2, s3 = call(pair_kernel, [(piece, BF)] * 4, (mine, other),
                           scratch=[pltpu.VMEM((V, K), BF)], name="pair")
    r1, r2, r3 = over_y((s1, s2, s3))
    r1, query = lax.optimization_barrier((r1, query))
    chips = [own, r1, r2, r3]
    row, = call(row_kernel, [(piece, BF)], chips, scratch=[pltpu.VMEM((4,) + piece, BF)], name="row")
    z1 = over_chips(row, lambda z, y: (z ^ 1, y))
    pair, = call(two_rows_kernel, [(piece, BF)], (row, z1), name="two_rows")
    z2 = over_chips(pair, lambda z, y: (z ^ 2, y))
    far1, far3 = to_row_4(pair, 1), to_row_4(pair, 3)
    own, s1, s2, s3 = call(spread_kernel, [(piece, BF)] * 4, (*chips, z1, far3, far1, z2),
                           scratch=[pltpu.VMEM((4,) + piece, BF)], name="spread")
    into, after = call(unpair_kernel, [(whole, BF)] * 2, (own, *over_y((s1, s2, s3)), other),
                       name="unpair")
    gated, s2 = call(
        back_kernel, [((rows, V), BF), ((rows, F), BF)],
        (after, swap(into), query, attn, gate, idc, w_out),
        flops=2 * rows * V * 768, name="back")
    p2 = over_tp(s2, 2)
    s1, s3 = call(beside_kernel, [((rows, F), BF)] * 2, (gated, w_out),
                  flops=4 * rows * V * F, name="beside")
    p1, p3 = over_tp(s1, 1), over_tp(s3, 3)
    own, = call(here_kernel, [((rows, F), F32)], (gated, w_out), flops=2 * rows * V * F, name="here")
    return (own + p1.astype(F32) + p2.astype(F32) + p3.astype(F32)).astype(BF)


def solution(mesh):
    return jax.shard_map(
        per_device,
        mesh=mesh,
        in_specs=(
            P("seq", "tp"),
            P(),
            P(None, "tp"),
            P(None, "tp"),
            P(None, "tp"),
            P(None, "tp"),
            P(),
            P(None, "tp"),
            P("tp"),
            P("tp"),
            P("tp", None),
            P("seq"),
        ),
        out_specs=P("seq", "tp"),
        check_vma=False,
    )
```

```python
import jax
import jax.numpy as jnp
from jax import lax
from jax.experimental import pallas as pl
from jax.experimental.pallas import tpu as pltpu
from jax.sharding import PartitionSpec as P

K = 256
V = 512
C = 64
F = 512
QUARTER = 128
META = 16
F32 = jnp.float32
BF = jnp.bfloat16
VM = pl.BlockSpec(memory_space=pltpu.VMEM)
HBM = pl.BlockSpec(memory_space=pltpu.HBM)


def dot(a, b, dims=((1,), (0,))):
    return lax.dot_general(a, b, (dims, ((), ())), preferred_element_type=F32)


def place():
    seq = lax.axis_index("seq")
    return lax.div(seq, 8), lax.rem(lax.div(seq, 2), 4), lax.rem(seq, 2)


def at(index, size):
    return pl.ds(pl.multiple_of(index * size, size), size)


FLIPS = (0, 2, 1, 3)


def flip(index, bits):
    return lax.bitwise_xor(index, bits)


def load(ref):
    rows = ref.shape[0] - META
    state = ref[0:rows].astype(F32)
    meta = ref[rows:].astype(F32)
    return state, meta[0:1] + meta[1:2], meta[2:3], meta[3:4]


def meta_of(decay, first, last):
    high = decay.astype(BF).astype(F32)
    row = lax.broadcasted_iota(jnp.int32, (META, K), 0)
    meta = jnp.where(row == 0, high, jnp.where(row == 1, decay - high, 0.0))
    meta = jnp.where(row == 2, first, jnp.where(row == 3, last, meta))
    return meta.astype(BF)


def save(ref, element):
    state, decay, first, last = element
    rows = state.shape[0]
    ref[0:rows] = state.astype(BF)
    ref[rows:] = meta_of(decay, first, last)


def joined(earlier, later):
    factor = jnp.where(later[2] == earlier[3], later[1], 0.0)
    return (later[0] + factor * earlier[0], factor * earlier[1], earlier[2], later[3])


def pick(cond, a, b):
    return jax.tree.map(lambda u, v: jnp.where(cond, u, v), a, b)


def block_cumsum(rate):
    row = lax.broadcasted_iota(jnp.int32, (4 * C, 4 * C), 0)
    col = lax.broadcasted_iota(jnp.int32, (4 * C, 4 * C), 1)
    mask = ((row >= col) & (row // C == col // C)).astype(BF)
    one = rate.astype(BF)
    rest = rate - one.astype(F32)
    two = rest.astype(BF)
    three = (rest - two.astype(F32)).astype(BF)
    return dot(mask, three) + dot(mask, two) + dot(mask, one)


def stage_kernel(*refs):
    count = len(refs) // 2
    done = refs[-1]
    copies = [pltpu.make_async_copy(refs[i], refs[count + i], done.at[i]) for i in range(count)]
    for copy in copies:
        copy.start()
    for copy in copies:
        copy.wait()


def front_kernel(t0, t1, t2, t3, gain, wk, wv, gd, gu, bias, idc,
                 normed, key_o, value_o, cum_o, element):
    x = lax.axis_index("tp")
    parts = [(ref, flip(x, d)) for d, ref in zip(FLIPS, (t0, t1, t2, t3))]
    squares = 0.0
    for ref, _ in parts:
        wide = ref[...].astype(F32)
        squares = squares + jnp.sum(wide * wide, axis=1, keepdims=True)
    scale = lax.rsqrt(squares * (1.0 / 2048) + 1e-05)
    key, value, low = 0.0, 0.0, 0.0
    for ref, owner in parts:
        part = (ref[...].astype(F32) * scale * gain[owner]).astype(BF)
        normed[owner] = part
        key = key + dot(part, wk[at(owner, F), :])
        value = value + dot(part, wv[at(owner, F), :])
        low = low + dot(part, gd[:, at(owner, F)], ((1,), (1,)))
    rate = dot(low.astype(BF), gu[...]) + bias[...]
    rate = (jnp.minimum(rate, 0.0) - jnp.log1p(jnp.exp(-jnp.abs(rate)))) * (1.0 / 16)
    key = key.astype(BF)
    key_o[...] = key
    value_o[...] = value.astype(BF)
    cum = block_cumsum(rate)
    cum_o[...] = cum
    ends = [cum[C * b + C - 1:C * b + C] for b in range(4)]
    after = [ends[1] + ends[2] + ends[3], ends[2] + ends[3], ends[3], jnp.zeros_like(ends[3])]
    ids = idc[...].astype(F32)
    first, last = ids[0:1], ids[4 * C - 1:]
    keep = (ids == last).astype(F32)
    ending = []
    for b in range(4):
        rows = slice(C * b, C * b + C)
        left = jnp.exp(after[b] + (ends[b] - cum[rows]))
        ending.append((key[rows].astype(F32) * left * keep[rows]).astype(BF))
    ending = jnp.concatenate(ending, axis=0)
    decay = jnp.exp(ends[0] + after[0])
    decay = jnp.where(first == last, decay, 0.0)
    element[0:V] = dot(value_o[...], ending, ((0,), (0,))).astype(BF)
    element[V:] = meta_of(decay, first, last)


def inner_kernel(normed, wq, wg, key_r, value_r, cum_r, idc, idr, head_gain,
                 query_o, attn_o, gate_o):
    query, gate = 0.0, 0.0
    for i in range(4):
        part = normed[i]
        query = query + dot(part, wq[i * F:(i + 1) * F, :])
        gate = gate + dot(part, wg[i * F:(i + 1) * F, :])
    gate_o[...] = gate / (1.0 + jnp.exp(-gate)) * head_gain[...]
    query = query.astype(BF).astype(F32) * (K ** -0.5)
    key = key_r[...].astype(F32)
    cum = cum_r[...]
    ends = [cum[C * b + C - 1:C * b + C] for b in range(4)]
    before = [jnp.zeros_like(ends[0])]
    for b in range(3):
        before.append(before[-1] + ends[b])
    total = [before[b] + cum[C * b:C * b + C] for b in range(4)]
    for b in range(4):
        rows = slice(C * b, C * b + C)
        query_o[rows] = (query[rows] * jnp.exp(total[b])).astype(BF)
        decayed = (query[rows] * jnp.exp(cum[rows])).astype(BF)
        keys = [(key[C * j:C * j + C] * jnp.exp(before[b] - total[j])).astype(BF) for j in range(b)]
        keys.append((key[rows] * jnp.exp(-cum[rows])).astype(BF))
        keys = jnp.concatenate(keys, axis=0)
        scores = dot(decayed, keys, ((1,), (1,)))
        row = lax.broadcasted_iota(jnp.int32, scores.shape, 0) + C * b
        col = lax.broadcasted_iota(jnp.int32, scores.shape, 1)
        allowed = (col <= row) & (idr[:, 0:C * b + C] == idc[rows])
        weights = jnp.where(allowed, scores, 0.0).astype(BF)
        attn_o[rows] = dot(weights, value_r[0:C * b + C])


def hold_kernel(a, b, c, d):
    c[...] = a[...]
    d[...] = b[...]


def at_middle():
    z, y, _ = place()
    return (z == 4) & (y == 0)


def pair_kernel(mine, other, own, s1, s2, s3, scratch):
    _, y, _ = place()
    total = joined(load(other), load(mine))
    scratch[...] = total[0].astype(BF)
    meta = meta_of(*total[1:])
    for d, ref in zip(FLIPS, (own, s1, s2, s3)):
        ref[0:QUARTER] = scratch[at(flip(y, d), QUARTER), :]
        ref[QUARTER:] = meta


def stack_rows(parts, stack):
    _, y, _ = place()
    for d, ref in zip(FLIPS, parts):
        stack[flip(y, d)] = ref[...]
    return [load(stack.at[i]) for i in range(4)]


def row_kernel(own, r1, r2, r3, total, stack):
    chips = stack_rows((own, r1, r2, r3), stack)
    run = chips[0]
    for chip in chips[1:]:
        run = joined(run, chip)
    save(total, run)


def two_rows_kernel(row, beside, total):
    z, _, _ = place()
    a, b = load(row), load(beside)
    odd = lax.rem(z, 2) == 1
    save(total, joined(pick(odd, b, a), pick(odd, a, b)))


def spread_kernel(own, r1, r2, r3, z1, z2, pair, own_o, s1, s2, s3, half, stack):
    z, y, _ = place()
    chips = stack_rows((own, r1, r2, r3), stack)
    other = load(z2)
    save(half, joined(other, load(pair)))
    before = (jnp.where(lax.rem(z, 4) >= 2, other[0], 0.0), *other[1:])
    run = pick(lax.rem(z, 2) == 1, joined(before, load(z1)), before)
    for i in range(4):
        save(stack.at[i], run)
        run = joined(run, chips[i])
    for d, ref in zip(FLIPS, (own_o, s1, s2, s3)):
        ref[...] = stack[flip(y, d)]


def unpair_kernel(own, far0, far2, r1, r2, r3, other, into, after):
    _, y, _ = place()
    for d, ref in zip(FLIPS, (own, r1, r2, r3)):
        into[at(flip(y, d), QUARTER), :] = ref[0:QUARTER]
    into[V:] = own[QUARTER:]
    save(after, joined(load(into), load(other)))

    @pl.when(at_middle())
    def _():
        into[QUARTER:2 * QUARTER] = far0[0:QUARTER]
        into[3 * QUARTER:V] = far2[0:QUARTER]


def back_kernel(after, into, far0, far2, query, attn_r, gate, idc, w_out, gated_o, s2, before):
    x = lax.axis_index("tp")
    _, _, c = place()
    before[...] = jnp.where(c == 0, into[...].astype(F32), after[...].astype(F32)).astype(BF)

    @pl.when(at_middle() & (c == 0))
    def _():
        before[0:QUARTER] = far0[0:QUARTER]
        before[2 * QUARTER:3 * QUARTER] = far2[0:QUARTER]
        before[V:] = far0[QUARTER:]

    seen = idc[...].astype(F32) == before[V:].astype(F32)[3:4, 0:1]
    inter = dot(query[...], before[0:V], ((1,), (1,)))
    full = attn_r[...] + jnp.where(seen, inter, 0.0)
    scale = lax.rsqrt(jnp.mean(full * full, axis=1, keepdims=True) + 1e-05)
    gated_o[...] = (full * scale * gate[...]).astype(BF)
    s2[...] = dot(gated_o[...], w_out[:, at(flip(x, 2), F)]).astype(BF)


def beside_kernel(gated, w_out, s1, s3):
    x = lax.axis_index("tp")
    for d, ref in ((3, s3), (1, s1)):
        ref[...] = dot(gated[...], w_out[:, at(flip(x, d), F)]).astype(BF)


def here_kernel(gated, w_out, own):
    x = lax.axis_index("tp")
    own[...] = dot(gated[...], w_out[:, at(x, F)])


def call(kernel, outs, args, specs=None, scratch=(), flops=0, name=None, vmem=24):
    shapes = [jax.ShapeDtypeStruct(s, d) for s, d in outs]
    bytes_accessed = sum(a.size * a.dtype.itemsize for a in list(args) + shapes)
    return pl.pallas_call(
        kernel,
        out_shape=shapes,
        in_specs=specs or [VM] * len(args),
        out_specs=[VM] * len(outs),
        scratch_shapes=list(scratch),
        compiler_params=pltpu.CompilerParams(vmem_limit_bytes=vmem << 20),
        cost_estimate=pl.CostEstimate(flops=flops, bytes_accessed=bytes_accessed, transcendentals=0),
        name=name,
    )(*args)


def over_tp(block, bits):
    return lax.ppermute(block, "tp", [(i, i ^ bits) for i in range(4)])


def over_seq(block, move):
    route = []
    for i in range(64):
        z, y, c = move(i // 8, i // 2 % 4, i % 2)
        route.append((i, z * 8 + y * 2 + c))
    return lax.ppermute(block, "seq", route)


def over_chips(block, move):
    route = []
    for i in range(256):
        z, y, c, x = i // 32, i // 8 % 4, i // 4 % 2, i % 4
        z, y, x = (*move(z, y), x) if c else (z, y, x ^ 1)
        route.append((i, ((z * 4 + y) * 2 + c) * 4 + x))
    return lax.ppermute(block, ("seq", "tp"), route)


def to_middle(block, y):
    pairs = {25 + 2 * (y + i): 32 + i for i in range(2)}
    pairs |= {b: a for a, b in pairs.items()}
    route = []
    for i in range(256):
        seq, x = i // 4, i % 4
        if seq not in pairs:
            seq, x = (seq, x ^ 1) if seq ^ 1 in pairs else (seq ^ 1, x)
        else:
            seq = pairs[seq]
        route.append((i, seq * 4 + x))
    return lax.ppermute(block, ("seq", "tp"), route)


def over_y(blocks):
    return [
        over_chips(b, lambda z, y, d=d: (z, y ^ d)) for d, b in zip(FLIPS[1:], blocks)
    ]


def swap(block):
    return over_seq(block, lambda z, y, c: (z, y, 1 - c))


def per_device(tokens, norm_gain, w_query, w_key, w_value, w_gate_out, gate_down, gate_up,
               gate_bias, head_gain, w_out, request_ids):
    rows = tokens.shape[0]
    t1, t2, t3 = (over_tp(tokens, d) for d in FLIPS[1:])
    idc, idr = request_ids.reshape(rows, 1), request_ids.reshape(1, rows)
    piece = (QUARTER + META, K)
    whole = (V + META, K)
    held = (tokens, norm_gain.reshape(4, 1, F), w_key, w_value, gate_down.T, gate_up,
            gate_bias.reshape(1, K))
    tokens, gain, w_key, w_value, down, up, bias = call(
        stage_kernel, [(a.shape, a.dtype) for a in held], held, specs=[HBM] * len(held),
        scratch=[pltpu.SemaphoreType.DMA((len(held),))], name="stage")
    normed, key, value, cum, mine = call(
        front_kernel,
        [((4, rows, F), BF), ((rows, K), BF), ((rows, V), BF), ((rows, K), F32), (whole, BF)],
        (tokens, t1, t2, t3, gain, w_key, w_value, down, up, bias, idc),
        flops=2 * rows * 2048 * 784, name="front")
    other = swap(mine)
    query, attn, gate = call(
        inner_kernel,
        [((rows, K), BF), ((rows, V), F32), ((rows, V), F32)],
        (normed, w_query, w_gate_out, key, value, cum, idc, idr, head_gain.reshape(1, V)),
        flops=2 * rows * 2048 * 1024, name="inner")
    own, s1, s2, s3 = call(pair_kernel, [(piece, BF)] * 4, (mine, other),
                           scratch=[pltpu.VMEM((V, K), BF)], name="pair")
    r1, r2, r3 = over_y((s1, s2, s3))
    chips = [own, r1, r2, r3]
    row, = call(row_kernel, [(piece, BF)], chips, scratch=[pltpu.VMEM((4,) + piece, BF)], name="row")
    z1 = over_chips(row, lambda z, y: (z ^ 1, y))
    z1, query = lax.optimization_barrier((z1, query))
    pair, = call(two_rows_kernel, [(piece, BF)], (row, z1), name="two_rows")
    z2 = over_chips(pair, lambda z, y: (z ^ 2, y))
    own, s1, s2, s3, half = call(spread_kernel, [(piece, BF)] * 5, (*chips, z1, z2, pair),
                                 scratch=[pltpu.VMEM((4,) + piece, BF)], name="spread")
    far0, far2 = call(hold_kernel, [(piece, BF)] * 2, (to_middle(half, 0), to_middle(half, 2)),
                      flops=2 * rows * V * 4096, name="hold")
    into, after = call(unpair_kernel, [(whole, BF)] * 2, (own, far0, far2, *over_y((s1, s2, s3)), other),
                       name="unpair")
    gated, s2 = call(
        back_kernel, [((rows, V), BF), ((rows, F), BF)],
        (after, swap(into), far0, far2, query, attn, gate, idc, w_out),
        scratch=[pltpu.VMEM(whole, BF)], flops=2 * rows * V * 768, name="back")
    p2 = over_tp(s2, 2)
    s1, s3 = call(beside_kernel, [((rows, F), BF)] * 2, (gated, w_out),
                  flops=4 * rows * V * F, name="beside")
    p1, p3 = over_tp(s1, 1), over_tp(s3, 3)
    own, = call(here_kernel, [((rows, F), F32)], (gated, w_out), flops=2 * rows * V * F, name="here")
    return (own + p1.astype(F32) + p2.astype(F32) + p3.astype(F32)).astype(BF)


def solution(mesh):
    return jax.shard_map(
        per_device,
        mesh=mesh,
        in_specs=(
            P("seq", "tp"),
            P(),
            P(None, "tp"),
            P(None, "tp"),
            P(None, "tp"),
            P(None, "tp"),
            P(),
            P(None, "tp"),
            P("tp"),
            P("tp"),
            P("tp", None),
            P("seq"),
        ),
        out_specs=P("seq", "tp"),
        check_vma=False,
    )
```

```python
import jax
import jax.numpy as jnp
from jax import lax
from jax.experimental import pallas as pl
from jax.experimental.pallas import tpu as pltpu
from jax.sharding import PartitionSpec as P

K = 256
V = 512
C = 64
F = 512
QUARTER = 128
META = 16
F32 = jnp.float32
BF = jnp.bfloat16
VM = pl.BlockSpec(memory_space=pltpu.VMEM)
HBM = pl.BlockSpec(memory_space=pltpu.HBM)


def dot(a, b, dims=((1,), (0,))):
    return lax.dot_general(a, b, (dims, ((), ())), preferred_element_type=F32)


def place():
    seq = lax.axis_index("seq")
    return lax.div(seq, 8), lax.rem(lax.div(seq, 2), 4), lax.rem(seq, 2)


def at(index, size):
    return pl.ds(pl.multiple_of(index * size, size), size)


FLIPS = (0, 2, 1, 3)
Y_FLIPS = (0, 1, 3, 2)


def flip(index, bits):
    return lax.bitwise_xor(index, bits)


def load(ref):
    rows = ref.shape[0] - META
    state = ref[0:rows].astype(F32)
    meta = ref[rows:].astype(F32)
    return state, meta[0:1] + meta[1:2], meta[2:3], meta[3:4]


def meta_of(decay, first, last):
    high = decay.astype(BF).astype(F32)
    row = lax.broadcasted_iota(jnp.int32, (META, K), 0)
    meta = jnp.where(row == 0, high, jnp.where(row == 1, decay - high, 0.0))
    meta = jnp.where(row == 2, first, jnp.where(row == 3, last, meta))
    return meta.astype(BF)


def save(ref, element):
    state, decay, first, last = element
    rows = state.shape[0]
    ref[0:rows] = state.astype(BF)
    ref[rows:] = meta_of(decay, first, last)


def joined(earlier, later):
    factor = jnp.where(later[2] == earlier[3], later[1], 0.0)
    return (later[0] + factor * earlier[0], factor * earlier[1], earlier[2], later[3])


def pick(cond, a, b):
    return jax.tree.map(lambda u, v: jnp.where(cond, u, v), a, b)


def block_cumsum(rate):
    row = lax.broadcasted_iota(jnp.int32, (4 * C, 4 * C), 0)
    col = lax.broadcasted_iota(jnp.int32, (4 * C, 4 * C), 1)
    mask = ((row >= col) & (row // C == col // C)).astype(BF)
    one = rate.astype(BF)
    rest = rate - one.astype(F32)
    two = rest.astype(BF)
    three = (rest - two.astype(F32)).astype(BF)
    return dot(mask, three) + dot(mask, two) + dot(mask, one)


def stage_kernel(*refs):
    count = len(refs) // 2
    done = refs[-1]
    copies = [pltpu.make_async_copy(refs[i], refs[count + i], done.at[i]) for i in range(count)]
    for copy in copies:
        copy.start()
    for copy in copies:
        copy.wait()


def front_kernel(t0, t1, t2, t3, gain, wk, wv, gd, gu, bias, idc,
                 normed, key_o, value_o, cum_o, element):
    x = lax.axis_index("tp")
    parts = [(ref, flip(x, d)) for d, ref in zip(FLIPS, (t0, t1, t2, t3))]
    squares = 0.0
    for ref, _ in parts:
        wide = ref[...].astype(F32)
        squares = squares + jnp.sum(wide * wide, axis=1, keepdims=True)
    scale = lax.rsqrt(squares * (1.0 / 2048) + 1e-05)
    key, value, low = 0.0, 0.0, 0.0
    for ref, owner in parts:
        part = (ref[...].astype(F32) * scale * gain[owner]).astype(BF)
        normed[owner] = part
        key = key + dot(part, wk[at(owner, F), :])
        value = value + dot(part, wv[at(owner, F), :])
        low = low + dot(part, gd[:, at(owner, F)], ((1,), (1,)))
    rate = dot(low.astype(BF), gu[...]) + bias[...]
    rate = (jnp.minimum(rate, 0.0) - jnp.log1p(jnp.exp(-jnp.abs(rate)))) * (1.0 / 16)
    key = key.astype(BF)
    key_o[...] = key
    value_o[...] = value.astype(BF)
    cum = block_cumsum(rate)
    cum_o[...] = cum
    ends = [cum[C * b + C - 1:C * b + C] for b in range(4)]
    after = [ends[1] + ends[2] + ends[3], ends[2] + ends[3], ends[3], jnp.zeros_like(ends[3])]
    ids = idc[...].astype(F32)
    first, last = ids[0:1], ids[4 * C - 1:]
    keep = (ids == last).astype(F32)
    ending = []
    for b in range(4):
        rows = slice(C * b, C * b + C)
        left = jnp.exp(after[b] + (ends[b] - cum[rows]))
        ending.append((key[rows].astype(F32) * left * keep[rows]).astype(BF))
    ending = jnp.concatenate(ending, axis=0)
    decay = jnp.exp(ends[0] + after[0])
    decay = jnp.where(first == last, decay, 0.0)
    element[0:V] = dot(value_o[...], ending, ((0,), (0,))).astype(BF)
    element[V:] = meta_of(decay, first, last)


def inner_kernel(normed, wq, wg, key_r, value_r, cum_r, idc, idr, head_gain,
                 query_o, attn_o, gate_o):
    query, gate = 0.0, 0.0
    for i in range(4):
        part = normed[i]
        query = query + dot(part, wq[i * F:(i + 1) * F, :])
        gate = gate + dot(part, wg[i * F:(i + 1) * F, :])
    gate_o[...] = gate / (1.0 + jnp.exp(-gate)) * head_gain[...]
    query = query.astype(BF).astype(F32) * (K ** -0.5)
    key = key_r[...].astype(F32)
    cum = cum_r[...]
    ends = [cum[C * b + C - 1:C * b + C] for b in range(4)]
    before = [jnp.zeros_like(ends[0])]
    for b in range(3):
        before.append(before[-1] + ends[b])
    total = [before[b] + cum[C * b:C * b + C] for b in range(4)]
    for b in range(4):
        rows = slice(C * b, C * b + C)
        query_o[rows] = (query[rows] * jnp.exp(total[b])).astype(BF)
        decayed = (query[rows] * jnp.exp(cum[rows])).astype(BF)
        keys = [(key[C * j:C * j + C] * jnp.exp(before[b] - total[j])).astype(BF) for j in range(b)]
        keys.append((key[rows] * jnp.exp(-cum[rows])).astype(BF))
        keys = jnp.concatenate(keys, axis=0)
        scores = dot(decayed, keys, ((1,), (1,)))
        row = lax.broadcasted_iota(jnp.int32, scores.shape, 0) + C * b
        col = lax.broadcasted_iota(jnp.int32, scores.shape, 1)
        allowed = (col <= row) & (idr[:, 0:C * b + C] == idc[rows])
        weights = jnp.where(allowed, scores, 0.0).astype(BF)
        attn_o[rows] = dot(weights, value_r[0:C * b + C])


def hold_kernel(a, b, c, d):
    c[...] = a[...]
    d[...] = b[...]


def at_middle():
    z, y, _ = place()
    return (z == 4) & (y == 0)


def pair_kernel(mine, other, own, s1, s2, s3, scratch):
    _, y, _ = place()
    total = joined(load(other), load(mine))
    scratch[...] = total[0].astype(BF)
    meta = meta_of(*total[1:])
    for d, ref in zip(Y_FLIPS, (own, s1, s2, s3)):
        ref[0:QUARTER] = scratch[at(flip(y, d), QUARTER), :]
        ref[QUARTER:] = meta


def stack_rows(parts, stack):
    _, y, _ = place()
    for d, ref in zip(Y_FLIPS, parts):
        stack[flip(y, d)] = ref[...]
    return [load(stack.at[i]) for i in range(4)]


def row_kernel(own, r1, r2, r3, total, stack):
    chips = stack_rows((own, r1, r2, r3), stack)
    run = chips[0]
    for chip in chips[1:]:
        run = joined(run, chip)
    save(total, run)


def two_rows_kernel(row, beside, total):
    z, _, _ = place()
    a, b = load(row), load(beside)
    odd = lax.rem(z, 2) == 1
    save(total, joined(pick(odd, b, a), pick(odd, a, b)))


def spread_kernel(own, r1, r2, r3, z1, z2, pair, own_o, s1, s2, s3, half, stack):
    z, y, _ = place()
    chips = stack_rows((own, r1, r2, r3), stack)
    other = load(z2)
    save(half, joined(other, load(pair)))
    before = (jnp.where(lax.rem(z, 4) >= 2, other[0], 0.0), *other[1:])
    run = pick(lax.rem(z, 2) == 1, joined(before, load(z1)), before)
    for i in range(4):
        save(stack.at[i], run)
        run = joined(run, chips[i])
    for d, ref in zip(Y_FLIPS, (own_o, s1, s2, s3)):
        ref[...] = stack[flip(y, d)]


def unpair_kernel(own, far0, far2, r1, r2, r3, other, into, after):
    _, y, _ = place()
    for d, ref in zip(Y_FLIPS, (own, r1, r2, r3)):
        into[at(flip(y, d), QUARTER), :] = ref[0:QUARTER]
    into[V:] = own[QUARTER:]
    save(after, joined(load(into), load(other)))

    @pl.when(at_middle())
    def _():
        into[QUARTER:2 * QUARTER] = far0[0:QUARTER]
        into[3 * QUARTER:V] = far2[0:QUARTER]


def back_kernel(after, into, far0, far2, query, attn_r, gate, idc, w_out, gated_o, s2, before):
    x = lax.axis_index("tp")
    _, _, c = place()
    before[...] = jnp.where(c == 0, into[...].astype(F32), after[...].astype(F32)).astype(BF)

    @pl.when(at_middle() & (c == 0))
    def _():
        before[0:QUARTER] = far0[0:QUARTER]
        before[2 * QUARTER:3 * QUARTER] = far2[0:QUARTER]
        before[V:] = far0[QUARTER:]

    seen = idc[...].astype(F32) == before[V:].astype(F32)[3:4, 0:1]
    inter = dot(query[...], before[0:V], ((1,), (1,)))
    full = attn_r[...] + jnp.where(seen, inter, 0.0)
    scale = lax.rsqrt(jnp.mean(full * full, axis=1, keepdims=True) + 1e-05)
    gated_o[...] = (full * scale * gate[...]).astype(BF)
    s2[...] = dot(gated_o[...], w_out[:, at(flip(x, 2), F)]).astype(BF)


def beside_kernel(gated, w_out, s1, s3):
    x = lax.axis_index("tp")
    for d, ref in ((3, s3), (1, s1)):
        ref[...] = dot(gated[...], w_out[:, at(flip(x, d), F)]).astype(BF)


def here_kernel(gated, w_out, own):
    x = lax.axis_index("tp")
    own[...] = dot(gated[...], w_out[:, at(x, F)])


def call(kernel, outs, args, specs=None, scratch=(), flops=0, name=None, vmem=24):
    shapes = [jax.ShapeDtypeStruct(s, d) for s, d in outs]
    bytes_accessed = sum(a.size * a.dtype.itemsize for a in list(args) + shapes)
    return pl.pallas_call(
        kernel,
        out_shape=shapes,
        in_specs=specs or [VM] * len(args),
        out_specs=[VM] * len(outs),
        scratch_shapes=list(scratch),
        compiler_params=pltpu.CompilerParams(vmem_limit_bytes=vmem << 20),
        cost_estimate=pl.CostEstimate(flops=flops, bytes_accessed=bytes_accessed, transcendentals=0),
        name=name,
    )(*args)


def over_tp(block, bits):
    return lax.ppermute(block, "tp", [(i, i ^ bits) for i in range(4)])


def over_seq(block, move):
    route = []
    for i in range(64):
        z, y, c = move(i // 8, i // 2 % 4, i % 2)
        route.append((i, z * 8 + y * 2 + c))
    return lax.ppermute(block, "seq", route)


def over_chips(block, move):
    route = []
    for i in range(256):
        z, y, c, x = i // 32, i // 8 % 4, i // 4 % 2, i % 4
        z, y, x = (*move(z, y), x) if c else (z, y, x ^ 1)
        route.append((i, ((z * 4 + y) * 2 + c) * 4 + x))
    return lax.ppermute(block, ("seq", "tp"), route)


def to_middle(block, y):
    pairs = {25 + 2 * (y + i): 32 + i for i in range(2)}
    pairs |= {b: a for a, b in pairs.items()}
    route = []
    for i in range(256):
        seq, x = i // 4, i % 4
        if seq not in pairs:
            seq, x = (seq, x ^ 1) if seq ^ 1 in pairs else (seq ^ 1, x)
        else:
            seq = pairs[seq]
        route.append((i, seq * 4 + x))
    return lax.ppermute(block, ("seq", "tp"), route)


def over_y(blocks):
    return [
        over_chips(b, lambda z, y, d=d: (z, y ^ d)) for d, b in zip(Y_FLIPS[1:], blocks)
    ]


def swap(block):
    return over_seq(block, lambda z, y, c: (z, y, 1 - c))


def per_device(tokens, norm_gain, w_query, w_key, w_value, w_gate_out, gate_down, gate_up,
               gate_bias, head_gain, w_out, request_ids):
    rows = tokens.shape[0]
    t1, t2, t3 = (over_tp(tokens, d) for d in FLIPS[1:])
    idc, idr = request_ids.reshape(rows, 1), request_ids.reshape(1, rows)
    piece = (QUARTER + META, K)
    whole = (V + META, K)
    held = (tokens, norm_gain.reshape(4, 1, F), w_key, w_value, gate_down.T, gate_up,
            gate_bias.reshape(1, K))
    tokens, gain, w_key, w_value, down, up, bias = call(
        stage_kernel, [(a.shape, a.dtype) for a in held], held, specs=[HBM] * len(held),
        scratch=[pltpu.SemaphoreType.DMA((len(held),))], name="stage")
    normed, key, value, cum, mine = call(
        front_kernel,
        [((4, rows, F), BF), ((rows, K), BF), ((rows, V), BF), ((rows, K), F32), (whole, BF)],
        (tokens, t1, t2, t3, gain, w_key, w_value, down, up, bias, idc),
        flops=2 * rows * 2048 * 784, name="front")
    other = swap(mine)
    query, attn, gate = call(
        inner_kernel,
        [((rows, K), BF), ((rows, V), F32), ((rows, V), F32)],
        (normed, w_query, w_gate_out, key, value, cum, idc, idr, head_gain.reshape(1, V)),
        flops=2 * rows * 2048 * 1024, name="inner")
    own, s1, s2, s3 = call(pair_kernel, [(piece, BF)] * 4, (mine, other),
                           scratch=[pltpu.VMEM((V, K), BF)], name="pair")
    r1, r2, r3 = over_y((s1, s2, s3))
    chips = [own, r1, r2, r3]
    row, = call(row_kernel, [(piece, BF)], chips, scratch=[pltpu.VMEM((4,) + piece, BF)], name="row")
    z1 = over_chips(row, lambda z, y: (z ^ 1, y))
    z1, query = lax.optimization_barrier((z1, query))
    pair, = call(two_rows_kernel, [(piece, BF)], (row, z1), name="two_rows")
    z2 = over_chips(pair, lambda z, y: (z ^ 2, y))
    own, s1, s2, s3, half = call(spread_kernel, [(piece, BF)] * 5, (*chips, z1, z2, pair),
                                 scratch=[pltpu.VMEM((4,) + piece, BF)], name="spread")
    far0, far2 = call(hold_kernel, [(piece, BF)] * 2, (to_middle(half, 0), to_middle(half, 2)),
                      flops=2 * rows * V * 4096, name="hold")
    into, after = call(unpair_kernel, [(whole, BF)] * 2, (own, far0, far2, *over_y((s1, s2, s3)), other),
                       name="unpair")
    gated, s2 = call(
        back_kernel, [((rows, V), BF), ((rows, F), BF)],
        (after, swap(into), far0, far2, query, attn, gate, idc, w_out),
        scratch=[pltpu.VMEM(whole, BF)], flops=2 * rows * V * 768, name="back")
    p2 = over_tp(s2, 2)
    s1, s3 = call(beside_kernel, [((rows, F), BF)] * 2, (gated, w_out),
                  flops=4 * rows * V * F, name="beside")
    p1, p3 = over_tp(s1, 1), over_tp(s3, 3)
    own, = call(here_kernel, [((rows, F), F32)], (gated, w_out), flops=2 * rows * V * F, name="here")
    return (own + p1.astype(F32) + p2.astype(F32) + p3.astype(F32)).astype(BF)


def solution(mesh):
    return jax.shard_map(
        per_device,
        mesh=mesh,
        in_specs=(
            P("seq", "tp"),
            P(),
            P(None, "tp"),
            P(None, "tp"),
            P(None, "tp"),
            P(None, "tp"),
            P(),
            P(None, "tp"),
            P("tp"),
            P("tp"),
            P("tp", None),
            P("seq"),
        ),
        out_specs=P("seq", "tp"),
        check_vma=False,
    )
```
